32 devices in a mesh: section: 8 (over z, x), dp: 4 (over y, core).
Axes of the slice: x: 2, y: 2, z: 4, core: 2. Of those that a mesh axis runs over, the one named last changes fastest.
Arguments:
- act_in: bfloat16 [8, 128, 2048], P('section', None, 'dp'), may hold values from -6 to 6
- saved_act: bfloat16 [8, 128, 2048], P('section', None, 'dp'), may hold values from -6 to 6
- cotangent: bfloat16 [8, 128, 2048], P('section', None, 'dp'), may hold values from -6 to 6
- weight_xz: bfloat16 [8, 2048, 8192], P('section', 'dp'), may hold values from -0.125 to 0.125
- weight_bcdt: bfloat16 [8, 320, 2048], P('section', None, 'dp'), may hold values from -0.125 to 0.125
- weight_out: bfloat16 [8, 4096, 2048], P('section', None, 'dp'), may hold values from -0.09375 to 0.09375
- conv_x: float32 [8, 4, 4096], P('section', None, 'dp'), may hold values from -3 to 3
- conv_bc: float32 [8, 4, 256], P('section'), may hold values from -3 to 3
- dt_bias: float32 [8, 64], P('section', 'dp'), may hold values from -8 to -2
- a_log: float32 [8, 64], P('section', 'dp'), may hold values from 0 to 2.7
- d_skip: float32 [8, 64], P('section', 'dp'), may hold values from 0.5 to 1.5
- norm_gain: float32 [8, 4096], P('section', 'dp'), may hold values from 0.1 to 1.9
Outputs:
- next_act: bfloat16 [8, 128, 2048], P('section', None, 'dp')
- prev_grad: bfloat16 [8, 128, 2048], P('section', None, 'dp')
- grad_xz: float32 [8, 2048, 8192], P('section', 'dp')
- grad_bcdt: float32 [8, 320, 2048], P('section', None, 'dp')
- grad_out: float32 [8, 4096, 2048], P('section', None, 'dp')
The draws below stay inside these ranges and needn't reach their ends.
All inputs are finite; a program needn't handle non-finite values.
Results may differ from the reference program's by a relative error of at most 0.0084.
Values may be sent and summed in bfloat16 or wider, within the bound.
A program may use at most 128 MiB of HBM per device.

```python
import jax
import jax.numpy as jnp
from jax import lax

D = 2048
HEAD_DIM = 64
NSTATE = 128
HEADS = 64
KCONV = 4
SEQ = 128
INNER = 4096
SECTIONS = 8


def levels(stream_key, dims, pieces, smallest, largest):
    def one(axis_at, parts):
        steps = jax.random.uniform(jax.random.fold_in(jax.random.fold_in(stream_key, 6), axis_at), (parts,), jnp.float32, smallest / len(pieces), largest / len(pieces))
        return jnp.repeat(jnp.exp(steps), dims[axis_at] // parts).reshape((-1,) + (1,) * (len(dims) - axis_at - 1))

    gain = one(*pieces[0])
    for cut in pieces[1:]:
        gain = gain * one(*cut)
    return gain


def bell_draw(own_key, shape, scale, limit, shards=(), kind=jnp.bfloat16):
    factor_of = levels(own_key, shape, shards, -0.22, 0.18) if shards else 1.0
    array = jax.random.normal(own_key, shape, jnp.float32) * scale * factor_of
    return jnp.minimum(jnp.maximum(array, -limit), limit).astype(kind)


def setup_inputs(seed: int = 0) -> dict:
    keys = jax.random.split(jax.random.key(seed), 13)
    act_in = bell_draw(keys[0], (SECTIONS, SEQ, D), 1.0, 6.0, ((0, 8), (2, 4)))
    saved_act = bell_draw(keys[1], (SECTIONS, SEQ, D), 1.0, 6.0, ((0, 8), (2, 4)))
    cotangent = bell_draw(keys[2], (SECTIONS, SEQ, D), 1.0, 6.0, ((0, 8), (2, 4)))
    weight_xz = bell_draw(keys[3], (SECTIONS, D, 2 * INNER), D ** -0.5, 0.125, ((0, 8), (1, 4)))
    weight_bcdt = bell_draw(keys[4], (SECTIONS, 2 * NSTATE + HEADS, D), D ** -0.5, 0.125, ((0, 8), (2, 4)))
    weight_out = bell_draw(keys[5], (SECTIONS, INNER, D), INNER ** -0.5, 0.09375, ((0, 8), (2, 4)))
    conv_x = bell_draw(keys[6], (SECTIONS, KCONV, INNER), KCONV ** -0.5, 3.0, ((0, 8), (2, 4)), jnp.float32)
    conv_bc = bell_draw(keys[7], (SECTIONS, KCONV, 2 * NSTATE), KCONV ** -0.5, 3.0, ((0, 8),), jnp.float32)
    dt_bias = jnp.clip(-8.0 + 6.0 * jax.random.uniform(keys[8], (SECTIONS, HEADS), jnp.float32) ** levels(keys[8], (SECTIONS, HEADS), ((0, 8), (1, 4)), -0.2, 0.2), -8.0, -2.0)
    a_log = jnp.clip(2.7 * jax.random.uniform(keys[9], (SECTIONS, HEADS), jnp.float32) ** levels(keys[9], (SECTIONS, HEADS), ((0, 8), (1, 4)), -0.2, 0.2), 0.0, 2.7)
    d_skip = jnp.clip(0.5 + 1.0 * jax.random.uniform(keys[10], (SECTIONS, HEADS), jnp.float32) ** levels(keys[10], (SECTIONS, HEADS), ((0, 8), (1, 4)), -0.2, 0.2), 0.5, 1.5)
    norm_gain = jnp.clip(1.0 + 0.18 * jax.random.normal(keys[11], (SECTIONS, INNER), jnp.float32), 0.1, 1.9)
    return dict(act_in=act_in, saved_act=saved_act, cotangent=cotangent, weight_xz=weight_xz, weight_bcdt=weight_bcdt, weight_out=weight_out, conv_x=conv_x, conv_bc=conv_bc, dt_bias=dt_bias, a_log=a_log, d_skip=d_skip, norm_gain=norm_gain)


def causal_conv(values, kernel_taps):
    kernel = kernel_taps.shape[0]
    length = values.shape[1]
    padded = jnp.pad(values, ((0, 0), (kernel - 1, 0), (0, 0)))
    running = jnp.zeros_like(values)
    for offset in range(kernel):
        running = running + kernel_taps[offset] * padded[:, offset:offset + length]
    return running

def map_scores(maps):
    input_map = maps[:, :, :NSTATE]
    output_map = maps[:, :, NSTATE:]
    return lax.dot_general(output_map, input_map, (((2,), (2,)), ((0,), (0,))), preferred_element_type=jnp.float32)

def map_grads(d_scores, maps):
    values = maps.astype(jnp.float32)
    input_map = values[:, :, :NSTATE]
    output_map = values[:, :, NSTATE:]
    d_input = jnp.einsum('bts,btn->bsn', d_scores, output_map, precision=lax.Precision.HIGHEST)
    d_output = jnp.einsum('bts,bsn->btn', d_scores, input_map, precision=lax.Precision.HIGHEST)
    return jnp.concatenate([d_input, d_output], axis=2)

def mixer(proj_x, proj_z, proj_dt, scores, conv_taps, dt_offset, log_rate, skip_gain):
    batch, length, width = proj_x.shape
    nheads = dt_offset.shape[0]
    head_width = width // nheads
    xconv = jax.nn.silu(causal_conv(proj_x, conv_taps))
    steps = jax.nn.softplus(proj_dt + dt_offset)
    cumul = jnp.cumsum(steps * -jnp.exp(log_rate), axis=1)
    position = jnp.arange(length)
    causal = (position[:, None] >= position[None, :])[None, None]
    heads_cum = jnp.swapaxes(cumul, 1, 2)
    spread = heads_cum[:, :, :, None] - heads_cum[:, :, None, :]
    decay = jnp.where(causal, jnp.exp(jnp.where(causal, spread, 0.0)), 0.0)
    weights = decay * scores[:, None] * jnp.swapaxes(steps, 1, 2)[:, :, None, :]
    heads_in = xconv.reshape(batch, length, nheads, head_width)
    result = jnp.einsum('bhts,bshp->bthp', weights, heads_in, precision=lax.Precision.HIGHEST)
    result = result + skip_gain[None, None, :, None] * heads_in
    gate_in = jax.nn.silu(proj_z.reshape(batch, length, nheads, head_width))
    return (result * gate_in).reshape(batch * length, width)

def project(rows, weight_xz, weight_bcdt, conv_bc):
    values = rows.astype(jnp.float32)
    scales = lax.rsqrt(lax.optimization_barrier(jnp.mean(values * values, axis=1, keepdims=True)) + 1e-05)
    normed = (values * scales).astype(jnp.bfloat16)
    proj_xz = jnp.dot(normed, weight_xz, preferred_element_type=jnp.float32)
    proj_bcdt = lax.dot_general(normed, weight_bcdt, (((1,), (1,)), ((), ())), preferred_element_type=jnp.float32)
    pre_maps = proj_bcdt[:, :2 * NSTATE]
    maps = jax.nn.silu(causal_conv(pre_maps[None], conv_bc))[0].astype(jnp.bfloat16)
    return (values, normed, scales, proj_xz, pre_maps, maps, proj_bcdt[:, 2 * NSTATE:])

def gate_parts(projected, conv_x, dt_bias, a_log, d_skip, norm_gain):
    values, normed, scales, proj_xz, pre_maps, maps, proj_dt = projected
    length = proj_xz.shape[0]
    split_xz = proj_xz.reshape(1, length, HEADS, 2, HEAD_DIM)
    mix_x = split_xz[:, :, :, 0].reshape(1, length, INNER)
    mix_z = split_xz[:, :, :, 1].reshape(1, length, INNER)
    maps_three = maps[None]
    scores = map_scores(maps_three)

    def local_mix(in_x, in_z, in_dt, in_scores):
        return mixer(in_x, in_z, in_dt, in_scores, conv_x, dt_bias, a_log, d_skip)
    gated, mix_back = jax.vjp(local_mix, mix_x, mix_z, proj_dt[None], scores)
    inverse = lax.rsqrt(lax.optimization_barrier(jnp.sum(gated * gated, axis=1)) / INNER + 1e-05)[:, None]
    mixed_in = (gated * inverse * norm_gain).astype(jnp.bfloat16)
    return (gated, mix_back, inverse, mixed_in, maps_three)

def one_section(packed):
    act_in, saved_act, cotangent, weight_xz, weight_bcdt, weight_out, conv_x, conv_bc, dt_bias, a_log, d_skip, norm_gain = packed
    forward_proj = project(act_in, weight_xz, weight_bcdt, conv_bc)
    mixed_in = gate_parts(forward_proj, conv_x, dt_bias, a_log, d_skip, norm_gain)[3]
    mixed = jnp.dot(mixed_in, weight_out, preferred_element_type=jnp.float32)
    section_out = (act_in.astype(jnp.float32) + mixed).astype(jnp.bfloat16)
    back_proj = project(saved_act, weight_xz, weight_bcdt, conv_bc)
    values, normed, scales, proj_xz, pre_maps, maps, proj_dt = back_proj
    gated, mix_back, inverse, mixed_in, maps_three = gate_parts(back_proj, conv_x, dt_bias, a_log, d_skip, norm_gain)
    length = values.shape[0]
    grad_out = jnp.dot(mixed_in.T, cotangent, preferred_element_type=jnp.float32)
    d_mixed = jnp.dot(cotangent, weight_out.T, preferred_element_type=jnp.float32)
    dots = lax.optimization_barrier(jnp.sum(d_mixed * norm_gain * gated, axis=1))
    d_gated = inverse * norm_gain * d_mixed - gated * (inverse * inverse * inverse) * dots[:, None] / INNER
    d_px, d_pz, d_pdt, d_scores = mix_back(d_gated)
    d_maps = map_grads(d_scores, maps_three)
    conv_out, conv_back = jax.vjp(lambda inner_v: jax.nn.silu(causal_conv(inner_v, conv_bc)), pre_maps[None])
    d_pre = conv_back(d_maps)[0][0]
    round_bcdt = jnp.concatenate([d_pre, d_pdt.reshape(length, HEADS)], axis=1).astype(jnp.bfloat16)
    round_xz = jnp.stack([d_px.reshape(length, HEADS, HEAD_DIM), d_pz.reshape(length, HEADS, HEAD_DIM)], axis=2).reshape(length, 2 * INNER).astype(jnp.bfloat16)
    grad_xz = jnp.dot(normed.T, round_xz, preferred_element_type=jnp.float32)
    grad_bcdt = jnp.dot(round_bcdt.T, normed, preferred_element_type=jnp.float32)
    d_normed = jnp.dot(round_xz, weight_xz.T, preferred_element_type=jnp.float32)
    d_normed = d_normed + jnp.dot(round_bcdt, weight_bcdt, preferred_element_type=jnp.float32)
    inner_sum = lax.optimization_barrier(jnp.sum(d_normed * values, axis=1, keepdims=True))
    d_norm_in = scales * d_normed - values * (scales * scales * scales) * inner_sum / D
    d_input = (cotangent.astype(jnp.float32) + d_norm_in).astype(jnp.bfloat16)
    return (section_out, d_input, grad_xz, grad_bcdt, grad_out)

def reference(act_in, saved_act, cotangent, weight_xz, weight_bcdt, weight_out, conv_x, conv_bc, dt_bias, a_log, d_skip, norm_gain):
    results = lax.map(one_section, (act_in, saved_act, cotangent, weight_xz, weight_bcdt, weight_out, conv_x, conv_bc, dt_bias, a_log, d_skip, norm_gain))
    section_out, d_input, grad_xz, grad_bcdt, grad_out = results
    next_act = jnp.roll(section_out, 1, axis=0)
    prev_grad = jnp.roll(d_input, -1, axis=0)
    return (next_act, prev_grad, grad_xz, grad_bcdt, grad_out)
```

```python
import jax
import jax.numpy as jnp
from jax import lax
from jax.sharding import PartitionSpec as P

D = 2048
HEAD_DIM = 64
NSTATE = 128
HEADS = 64
SEQ = 128
INNER = 4096
MAPS = 2 * NSTATE


def from_behind(x, axis, by):
    length = lax.axis_size(axis)
    return lax.ppermute(x, axis, [(i, (i + by) % length) for i in range(length)])


def swap(x, mask):
    length = lax.axis_size("dp")
    return lax.ppermute(x, "dp", [(i, i ^ mask) for i in range(length)])


def masks():
    length = lax.axis_size("dp")
    out = []
    bit = 1
    while bit < length:
        out.append(bit)
        bit *= 2
    return out


def sum_all(x):
    for bit in masks():
        x = x + swap(x, bit)
    return x


def sum_scatter(part):
    length = lax.axis_size("dp")
    held = None
    for bit in masks():
        live = [j for j in range(0, length, bit)]
        away = [j for j in live if j & bit]
        home = [j for j in live if not j & bit]
        if held is None:
            sent = [part(j).astype(jnp.bfloat16) for j in away]
        else:
            sent = [held[j].astype(jnp.bfloat16) for j in away]
        came = [swap(s, bit) for s in sent]
        if held is None:
            held = {j: part(j) for j in home}
        held = {j: held[j] + c.astype(jnp.float32) for j, c in zip(home, came)}
    return held[0]


def gather_cols(block):
    me = lax.axis_index("dp")
    rows, width = block.shape
    length = lax.axis_size("dp")
    held = [block]
    for bit in reversed(masks()):
        held = held + [swap(b, bit) for b in held]
    order = [0]
    for bit in reversed(masks()):
        order = order + [j ^ bit for j in order]
    by_mask = {j: b for j, b in zip(order, held)}
    level = [by_mask[j] for j in range(length)]
    for bit in masks():
        flip = (me & bit) != 0
        level = [jnp.where(flip, level[j ^ bit], level[j]) for j in range(length)]
    return jnp.concatenate(level, axis=1)


def causal_conv(values, kernel_taps):
    kernel = kernel_taps.shape[0]
    length = values.shape[0]
    padded = jnp.pad(values, ((kernel - 1, 0), (0, 0)))
    running = jnp.zeros_like(values)
    for offset in range(kernel):
        running = running + kernel_taps[offset] * padded[offset : offset + length]
    return running


def mixer(proj_x, proj_z, proj_dt, scores, conv_taps, dt_offset, log_rate, skip_gain):
    length, width = proj_x.shape
    nheads = dt_offset.shape[0]
    head_width = width // nheads
    xconv = jax.nn.silu(causal_conv(proj_x, conv_taps))
    steps = jax.nn.softplus(proj_dt + dt_offset)
    position = jnp.arange(length)
    causal = position[:, None] >= position[None, :]
    cumul = jnp.dot(
        causal.astype(jnp.float32), steps * -jnp.exp(log_rate), precision=lax.Precision.HIGHEST
    )
    heads_cum = cumul.T
    spread = heads_cum[:, :, None] - heads_cum[:, None, :]
    decay = jnp.where(causal[None], jnp.exp(jnp.where(causal[None], spread, 0.0)), 0.0)
    weights = decay * scores[None] * steps.T[:, None, :]
    heads_in = xconv.reshape(length, nheads, head_width)
    result = jnp.einsum("hts,shp->thp", weights, heads_in, precision=lax.Precision.HIGH)
    result = result + skip_gain[None, :, None] * heads_in
    gate_in = jax.nn.silu(proj_z.reshape(length, nheads, head_width))
    return (result * gate_in).reshape(length, width)


def times_transposed(left, right):
    return lax.dot_general(
        left, right, (((1,), (1,)), ((), ())), preferred_element_type=jnp.float32
    )


def transposed_times(left, right):
    return lax.dot_general(
        left, right, (((0,), (0,)), ((), ())), preferred_element_type=jnp.float32
    )


def per_device(
    act_in,
    saved_act,
    cotangent,
    weight_xz,
    weight_bcdt,
    weight_out,
    conv_x,
    conv_bc,
    dt_bias,
    a_log,
    d_skip,
    norm_gain,
):
    input_rows = act_in[0]
    saved_rows = saved_act[0]
    cot_rows = cotangent[0]
    local_xz = weight_xz[0]
    local_bcdt = weight_bcdt[0]
    local_out = weight_out[0]
    taps_x = conv_x[0]
    taps_bc = conv_bc[0]
    dt_offset = dt_bias[0]
    log_rate = a_log[0]
    skip_gain = d_skip[0]
    gain_local = norm_gain[0]
    own_heads = dt_offset.shape[0]
    me = lax.axis_index("dp")
    head_first = me * own_heads
    width = own_heads * HEAD_DIM

    def whole_act(pre_part):
        return jax.nn.silu(causal_conv(pre_part, taps_bc))

    def project(rows):
        values = rows.astype(jnp.float32)
        squares = jnp.sum(values * values, axis=1, keepdims=True)

        def part(j):
            cols = lax.dynamic_slice_in_dim(local_xz, (me ^ j) * 2 * width, 2 * width, 1)
            return jnp.dot(rows, cols, preferred_element_type=jnp.float32)

        raw_xz = sum_scatter(part)
        small = sum_all(jnp.concatenate([times_transposed(rows, local_bcdt), squares], axis=1))
        raw_cols = small[:, : MAPS + HEADS]
        scales = lax.rsqrt(small[:, MAPS + HEADS :] / D + 1e-05)
        return (values, scales, raw_xz, raw_cols)

    def gate_parts(projected):
        values, scales, raw_xz, raw_cols = projected
        own_xz = raw_xz * scales
        whole_cols = raw_cols * scales
        pre_part = whole_cols[:, :MAPS]
        maps = whole_act(pre_part).astype(jnp.bfloat16)
        own_dt = lax.dynamic_slice_in_dim(whole_cols[:, MAPS:], head_first, own_heads, 1)
        split_xz = own_xz.reshape(SEQ, own_heads, 2, HEAD_DIM)
        mix_x = split_xz[:, :, 0].reshape(SEQ, width)
        mix_z = split_xz[:, :, 1].reshape(SEQ, width)
        scores = times_transposed(maps[:, NSTATE:], maps[:, :NSTATE])

        def local_mix(in_x, in_z, in_dt, in_scores):
            return mixer(in_x, in_z, in_dt, in_scores, taps_x, dt_offset, log_rate, skip_gain)

        gated, mix_back = jax.vjp(local_mix, mix_x, mix_z, own_dt, scores)
        return (gated, mix_back, maps, pre_part)

    back_proj = project(saved_rows)

    def mixed_part(j):
        taken = lax.dynamic_slice_in_dim(local_out, (me ^ j) * width, width, 0)
        return times_transposed(cot_rows, taken)

    d_mixed = sum_scatter(mixed_part)
    forward_proj = project(input_rows)

    values, scales, raw_xz, raw_cols = back_proj
    gated, mix_back, maps, pre_part = gate_parts(back_proj)
    gained = gated * gain_local
    row_sums = sum_all(
        jnp.stack([jnp.sum(gated * gated, axis=1), jnp.sum(d_mixed * gained, axis=1)])
    )
    inverse = lax.rsqrt(row_sums[0] / INNER + 1e-05)[:, None]
    dots = row_sums[1][:, None]
    mixed_in = (gained * inverse).astype(jnp.bfloat16)
    d_gated = inverse * gain_local * d_mixed - gated * (inverse * inverse * inverse) * dots / INNER
    d_px, d_pz, d_pdt, d_scores = mix_back(d_gated)
    own_round = (
        jnp.stack(
            [
                d_px.reshape(SEQ, own_heads, HEAD_DIM),
                d_pz.reshape(SEQ, own_heads, HEAD_DIM),
            ],
            axis=2,
        )
        .reshape(SEQ, own_heads * 2 * HEAD_DIM)
        .astype(jnp.bfloat16)
    )
    round_xz = gather_cols(own_round)
    inner_own = jnp.sum(own_round.astype(jnp.float32) * raw_xz, axis=1, keepdims=True)
    wide_maps = maps.astype(jnp.float32)
    d_maps = jnp.concatenate(
        [
            jnp.dot(d_scores.T, wide_maps[:, NSTATE:], precision=lax.Precision.HIGH),
            jnp.dot(d_scores, wide_maps[:, :NSTATE], precision=lax.Precision.HIGH),
        ],
        axis=1,
    )
    d_dt_full = lax.dynamic_update_slice_in_dim(
        jnp.zeros((SEQ, HEADS), jnp.float32), d_pdt, head_first, 1
    )
    summed = sum_all(jnp.concatenate([d_maps, d_dt_full, inner_own], axis=1))
    conv_out, conv_back = jax.vjp(whole_act, pre_part)
    d_pre = conv_back(summed[:, :MAPS])[0]
    round_bcdt = jnp.concatenate([d_pre, summed[:, MAPS : MAPS + HEADS]], axis=1).astype(
        jnp.bfloat16
    )
    inner_sum = summed[:, MAPS + HEADS :] + jnp.sum(
        round_bcdt.astype(jnp.float32) * raw_cols, axis=1, keepdims=True
    )

    fwd_gated = gate_parts(forward_proj)[0]
    fwd_all = gather_cols((fwd_gated * gain_local).astype(jnp.bfloat16))
    fwd_sum = sum_all(jnp.sum(fwd_gated * fwd_gated, axis=1)[None])
    fwd_inverse = lax.rsqrt(fwd_sum[0] / INNER + 1e-05)[:, None]
    mixed = jnp.dot(fwd_all, local_out, preferred_element_type=jnp.float32) * fwd_inverse
    section_out = (input_rows.astype(jnp.float32) + mixed).astype(jnp.bfloat16)
    next_act = from_behind(section_out, "section", 1)

    normed = (values * scales).astype(jnp.bfloat16)
    d_normed = times_transposed(round_xz, local_xz)
    d_normed = d_normed + jnp.dot(round_bcdt, local_bcdt, preferred_element_type=jnp.float32)
    d_norm_in = scales * d_normed - values * (scales * scales * scales) * inner_sum / D
    d_input = (cot_rows.astype(jnp.float32) + d_norm_in).astype(jnp.bfloat16)
    prev_grad = from_behind(d_input, "section", -1)

    grad_out = transposed_times(gather_cols(mixed_in), cot_rows)
    grad_xz = transposed_times(normed, round_xz)
    grad_bcdt = transposed_times(round_bcdt, normed)
    return (next_act[None], prev_grad[None], grad_xz[None], grad_bcdt[None], grad_out[None])


def solution(mesh):
    return jax.shard_map(
        per_device,
        mesh=mesh,
        in_specs=(
            P("section", None, "dp"),
            P("section", None, "dp"),
            P("section", None, "dp"),
            P("section", "dp", None),
            P("section", None, "dp"),
            P("section", None, "dp"),
            P("section", None, "dp"),
            P("section", None, None),
            P("section", "dp"),
            P("section", "dp"),
            P("section", "dp"),
            P("section", "dp"),
        ),
        out_specs=(
            P("section", None, "dp"),
            P("section", None, "dp"),
            P("section", "dp", None),
            P("section", None, "dp"),
            P("section", None, "dp"),
        ),
        check_vma=False,
    )
```

```python
import functools

import jax
import jax.numpy as jnp
from jax import lax
from jax.experimental import pallas as pl
from jax.experimental.pallas import tpu as pltpu
from jax.sharding import PartitionSpec as P

D = 2048
HEAD_DIM = 64
NSTATE = 128
HEADS = 64
SEQ = 128
INNER = 4096
MAPS = 2 * NSTATE


def from_behind(x, axis, by):
    length = lax.axis_size(axis)
    return lax.ppermute(x, axis, [(i, (i + by) % length) for i in range(length)])


def swap(x, mask):
    length = lax.axis_size("dp")
    return lax.ppermute(x, "dp", [(i, i ^ mask) for i in range(length)])


def masks():
    length = lax.axis_size("dp")
    out = []
    bit = 1
    while bit < length:
        out.append(bit)
        bit *= 2
    return out


def sum_all(x):
    for bit in masks():
        x = x + swap(x, bit)
    return x


def parts_body(counts, transposed, me_ref, *refs):
    streams, addends = counts
    rows = refs[0][...]
    weights = refs[1][...]
    contract = 1 if transposed else 0
    product = lax.dot_general(
        rows, weights, (((1,), (contract,)), ((), ())), preferred_element_type=jnp.float32
    )
    outs = refs[2 + addends :]
    for at in range(streams):
        term = product[at * SEQ : (at + 1) * SEQ]
        if addends:
            term = term + refs[2 + at][0].astype(jnp.float32)
        outs[at][0] = term.astype(outs[at].dtype)


def parts(me, rows, weights, first, step, added, kind, transposed, name):
    length = lax.axis_size("dp")
    count = (length - first + step - 1) // step
    streams = rows.shape[0] // SEQ
    depth = rows.shape[1]
    total = weights.shape[0] if transposed else weights.shape[1]
    chunk = total // length
    tile = min(1024, chunk)
    tiles = chunk // tile

    def block_at(g, t, me_ref):
        return (me_ref[0] ^ (first + step * g)) * tiles + t

    if transposed:
        weight_spec = pl.BlockSpec((tile, depth), lambda g, t, me_ref: (block_at(g, t, me_ref), 0))
    else:
        weight_spec = pl.BlockSpec((depth, tile), lambda g, t, me_ref: (0, block_at(g, t, me_ref)))
    stack_spec = pl.BlockSpec((1, SEQ, tile), lambda g, t, me_ref: (g, 0, t))
    size = jnp.dtype(kind).itemsize
    return pl.pallas_call(
        functools.partial(parts_body, (streams, len(added)), transposed),
        grid_spec=pltpu.PrefetchScalarGridSpec(
            num_scalar_prefetch=1,
            grid=(count, tiles),
            in_specs=[pl.BlockSpec(rows.shape, lambda g, t, me_ref: (0, 0)), weight_spec]
            + [stack_spec] * len(added),
            out_specs=[stack_spec] * streams,
        ),
        out_shape=[jax.ShapeDtypeStruct((count, SEQ, chunk), kind)] * streams,
        cost_estimate=pl.CostEstimate(
            flops=2 * rows.shape[0] * depth * chunk * count,
            bytes_accessed=count * chunk * (2 * depth + streams * SEQ * size),
            transcendentals=0,
        ),
        name=name,
    )(me, rows, weights, *added)


def grad_body(left_ref, right_ref, out_ref):
    out_ref[0] = lax.dot_general(
        left_ref[...],
        right_ref[...],
        (((0,), (0,)), ((), ())),
        preferred_element_type=jnp.float32,
    )


def weight_grad(left, right, by_rows, name):
    length, high = left.shape
    wide = right.shape[1]
    if by_rows:
        tile = min(1024, high)
        grid = (high // tile,)
        specs = [
            pl.BlockSpec((length, tile), lambda t: (0, t)),
            pl.BlockSpec((length, wide), lambda t: (0, 0)),
        ]
        out_spec = pl.BlockSpec((1, tile, wide), lambda t: (0, t, 0))
    else:
        tile = min(1024, wide)
        grid = (wide // tile,)
        specs = [
            pl.BlockSpec((length, high), lambda t: (0, 0)),
            pl.BlockSpec((length, tile), lambda t: (0, t)),
        ]
        out_spec = pl.BlockSpec((1, high, tile), lambda t: (0, 0, t))
    return pl.pallas_call(
        grad_body,
        grid=grid,
        in_specs=specs,
        out_specs=out_spec,
        out_shape=jax.ShapeDtypeStruct((1, high, wide), jnp.float32),
        cost_estimate=pl.CostEstimate(
            flops=2 * length * high * wide,
            bytes_accessed=4 * high * wide,
            transcendentals=0,
        ),
        name=name,
    )(left, right)


def tied(x, other):
    return lax.optimization_barrier((x, other))[0]


def first_swaps(stacks):
    return [swap(s, 1) for s in stacks]


def gather_cols(block):
    me = lax.axis_index("dp")
    rows, width = block.shape
    length = lax.axis_size("dp")
    held = [block]
    for bit in reversed(masks()):
        held = held + [swap(b, bit) for b in held]
    order = [0]
    for bit in reversed(masks()):
        order = order + [j ^ bit for j in order]
    by_mask = {j: b for j, b in zip(order, held)}
    level = [by_mask[j] for j in range(length)]
    for bit in masks():
        flip = (me & bit) != 0
        level = [jnp.where(flip, level[j ^ bit], level[j]) for j in range(length)]
    return jnp.concatenate(level, axis=1)


def causal_conv(values, kernel_taps):
    kernel = kernel_taps.shape[0]
    length = values.shape[0]
    padded = jnp.pad(values, ((kernel - 1, 0), (0, 0)))
    running = jnp.zeros_like(values)
    for offset in range(kernel):
        running = running + kernel_taps[offset] * padded[offset : offset + length]
    return running


def mixer(proj_x, proj_z, proj_dt, scores, conv_taps, dt_offset, log_rate, skip_gain):
    length, width = proj_x.shape
    nheads = dt_offset.shape[0]
    head_width = width // nheads
    xconv = jax.nn.silu(causal_conv(proj_x, conv_taps))
    steps = jax.nn.softplus(proj_dt + dt_offset)
    position = jnp.arange(length)
    causal = position[:, None] >= position[None, :]
    cumul = jnp.dot(
        causal.astype(jnp.float32), steps * -jnp.exp(log_rate), precision=lax.Precision.HIGHEST
    )
    heads_cum = cumul.T
    spread = heads_cum[:, :, None] - heads_cum[:, None, :]
    decay = jnp.where(causal[None], jnp.exp(jnp.where(causal[None], spread, 0.0)), 0.0)
    weights = decay * scores[None] * steps.T[:, None, :]
    heads_in = xconv.reshape(length, nheads, head_width)
    result = jnp.einsum("hts,shp->thp", weights, heads_in, precision=lax.Precision.HIGH)
    result = result + skip_gain[None, :, None] * heads_in
    gate_in = jax.nn.silu(proj_z.reshape(length, nheads, head_width))
    return (result * gate_in).reshape(length, width)


def times_transposed(left, right):
    return lax.dot_general(
        left, right, (((1,), (1,)), ((), ())), preferred_element_type=jnp.float32
    )


def transposed_times(left, right):
    return lax.dot_general(
        left, right, (((0,), (0,)), ((), ())), preferred_element_type=jnp.float32
    )


def per_device(
    act_in,
    saved_act,
    cotangent,
    weight_xz,
    weight_bcdt,
    weight_out,
    conv_x,
    conv_bc,
    dt_bias,
    a_log,
    d_skip,
    norm_gain,
):
    input_rows = act_in[0]
    saved_rows = saved_act[0]
    cot_rows = cotangent[0]
    local_xz = weight_xz[0]
    local_bcdt = weight_bcdt[0]
    local_out = weight_out[0]
    taps_x = conv_x[0]
    taps_bc = conv_bc[0]
    dt_offset = dt_bias[0]
    log_rate = a_log[0]
    skip_gain = d_skip[0]
    gain_local = norm_gain[0]
    own_heads = dt_offset.shape[0]
    me = lax.axis_index("dp")
    head_first = me * own_heads
    width = own_heads * HEAD_DIM

    def whole_act(pre_part):
        return jax.nn.silu(causal_conv(pre_part, taps_bc))

    me_one = jnp.full((1,), me, jnp.int32)
    length = lax.axis_size("dp")
    both = jnp.concatenate([saved_rows, input_rows], axis=0)
    xz_away = parts(me_one, both, local_xz, 1, 2, [], jnp.bfloat16, False, "xz_away")
    xz_came = first_swaps(xz_away)
    out_away = parts(me_one, cot_rows, local_out, 1, 2, [], jnp.bfloat16, True, "out_away")
    out_came = first_swaps(out_away)
    both_values = both.astype(jnp.float32)
    squares = jnp.sum(both_values * both_values, axis=1, keepdims=True)
    small = sum_all(jnp.concatenate([times_transposed(both, local_bcdt), squares], axis=1))

    def later(stack_came, rows, weights, transposed, name):
        sent = None
        if length > 2:
            sent = parts(
                me_one, rows, weights, 2, 4, [c[1::2] for c in stack_came], jnp.bfloat16, transposed, name + "_send"
            )
        kept = parts(
            me_one, rows, weights, 0, 4, [c[0::2] for c in stack_came], jnp.float32,
            transposed, name + "_keep"
        )
        return sent, kept

    def finish(kept, came):
        held = kept if came is None else kept + came.astype(jnp.float32)
        bit = 4
        held = {4 * k: held[k] for k in range(held.shape[0])}
        while bit < length:
            held = {
                j: held[j] + swap(held[j ^ bit].astype(jnp.bfloat16), bit).astype(jnp.float32)
                for j in held
                if not j & bit
            }
            bit *= 2
        return held[0]

    xz_sent, xz_kept = later(xz_came, both, local_xz, False, "xz")
    out_sent, out_kept = later(out_came, cot_rows, local_out, True, "out")
    back_came = forward_came = mixed_came = None
    if xz_sent is not None:
        back_came = swap(xz_sent[0], 2)
        mixed_came = swap(out_sent[0], 2)
        forward_came = swap(tied(xz_sent[1], back_came), 2)
    back_raw = finish(xz_kept[0], back_came)
    d_mixed = finish(out_kept[0], mixed_came)
    forward_raw = finish(xz_kept[1], forward_came)

    def project(rows, own_small, raw_xz):
        raw_cols = own_small[:, : MAPS + HEADS]
        scales = lax.rsqrt(own_small[:, MAPS + HEADS :] / D + 1e-05)
        return (rows.astype(jnp.float32), scales, raw_xz, raw_cols)

    back_proj = project(saved_rows, small[:SEQ], back_raw)
    forward_proj = project(input_rows, small[SEQ:], forward_raw)

    def gate_parts(projected):
        values, scales, raw_xz, raw_cols = projected
        own_xz = raw_xz * scales
        whole_cols = raw_cols * scales
        pre_part = whole_cols[:, :MAPS]
        maps = whole_act(pre_part).astype(jnp.bfloat16)
        own_dt = lax.dynamic_slice_in_dim(whole_cols[:, MAPS:], head_first, own_heads, 1)
        split_xz = own_xz.reshape(SEQ, own_heads, 2, HEAD_DIM)
        mix_x = split_xz[:, :, 0].reshape(SEQ, width)
        mix_z = split_xz[:, :, 1].reshape(SEQ, width)
        scores = times_transposed(maps[:, NSTATE:], maps[:, :NSTATE])

        def local_mix(in_x, in_z, in_dt, in_scores):
            return mixer(in_x, in_z, in_dt, in_scores, taps_x, dt_offset, log_rate, skip_gain)

        gated, mix_back = jax.vjp(local_mix, mix_x, mix_z, own_dt, scores)
        return (gated, mix_back, maps, pre_part)

    values, scales, raw_xz, raw_cols = back_proj
    gated, mix_back, maps, pre_part = gate_parts(back_proj)
    gained = gated * gain_local
    row_sums = sum_all(
        jnp.stack([jnp.sum(gated * gated, axis=1), jnp.sum(d_mixed * gained, axis=1)])
    )
    inverse = lax.rsqrt(row_sums[0] / INNER + 1e-05)[:, None]
    dots = row_sums[1][:, None]
    mixed_in = (gained * inverse).astype(jnp.bfloat16)
    d_gated = inverse * gain_local * d_mixed - gated * (inverse * inverse * inverse) * dots / INNER
    d_px, d_pz, d_pdt, d_scores = mix_back(d_gated)
    own_round = (
        jnp.stack(
            [
                d_px.reshape(SEQ, own_heads, HEAD_DIM),
                d_pz.reshape(SEQ, own_heads, HEAD_DIM),
            ],
            axis=2,
        )
        .reshape(SEQ, own_heads * 2 * HEAD_DIM)
        .astype(jnp.bfloat16)
    )
    round_xz = gather_cols(own_round)
    inner_own = jnp.sum(own_round.astype(jnp.float32) * raw_xz, axis=1, keepdims=True)
    wide_maps = maps.astype(jnp.float32)
    d_maps = jnp.concatenate(
        [
            jnp.dot(d_scores.T, wide_maps[:, NSTATE:], precision=lax.Precision.HIGH),
            jnp.dot(d_scores, wide_maps[:, :NSTATE], precision=lax.Precision.HIGH),
        ],
        axis=1,
    )
    d_dt_full = lax.dynamic_update_slice_in_dim(
        jnp.zeros((SEQ, HEADS), jnp.float32), d_pdt, head_first, 1
    )
    summed = sum_all(jnp.concatenate([d_maps, d_dt_full, inner_own], axis=1))
    conv_out, conv_back = jax.vjp(whole_act, pre_part)
    d_pre = conv_back(summed[:, :MAPS])[0]
    round_bcdt = jnp.concatenate([d_pre, summed[:, MAPS : MAPS + HEADS]], axis=1).astype(
        jnp.bfloat16
    )
    inner_sum = summed[:, MAPS + HEADS :] + jnp.sum(
        round_bcdt.astype(jnp.float32) * raw_cols, axis=1, keepdims=True
    )

    fwd_gated = gate_parts(forward_proj)[0]
    fwd_all = gather_cols((fwd_gated * gain_local).astype(jnp.bfloat16))
    fwd_sum = sum_all(jnp.sum(fwd_gated * fwd_gated, axis=1)[None])
    fwd_inverse = lax.rsqrt(fwd_sum[0] / INNER + 1e-05)[:, None]
    mixed = jnp.dot(fwd_all, local_out, preferred_element_type=jnp.float32) * fwd_inverse
    section_out = (input_rows.astype(jnp.float32) + mixed).astype(jnp.bfloat16)
    next_act = from_behind(section_out, "section", 1)

    normed = (values * scales).astype(jnp.bfloat16)
    d_normed = times_transposed(round_xz, local_xz)
    d_normed = d_normed + jnp.dot(round_bcdt, local_bcdt, preferred_element_type=jnp.float32)
    d_norm_in = scales * d_normed - values * (scales * scales * scales) * inner_sum / D
    d_input = (cot_rows.astype(jnp.float32) + d_norm_in).astype(jnp.bfloat16)
    prev_grad = from_behind(d_input, "section", -1)

    grad_out = weight_grad(gather_cols(mixed_in), cot_rows, True, "grad_out")
    grad_xz = weight_grad(normed, round_xz, False, "grad_xz")
    grad_bcdt = transposed_times(round_bcdt, normed)
    return (next_act[None], prev_grad[None], grad_xz, grad_bcdt[None], grad_out)


def solution(mesh):
    return jax.shard_map(
        per_device,
        mesh=mesh,
        in_specs=(
            P("section", None, "dp"),
            P("section", None, "dp"),
            P("section", None, "dp"),
            P("section", "dp", None),
            P("section", None, "dp"),
            P("section", None, "dp"),
            P("section", None, "dp"),
            P("section", None, None),
            P("section", "dp"),
            P("section", "dp"),
            P("section", "dp"),
            P("section", "dp"),
        ),
        out_specs=(
            P("section", None, "dp"),
            P("section", None, "dp"),
            P("section", "dp", None),
            P("section", None, "dp"),
            P("section", None, "dp"),
        ),
        check_vma=False,
    )
```

```python
import jax
import jax.numpy as jnp
from jax import lax
from jax.sharding import PartitionSpec as P

D = 2048
HEAD_DIM = 64
NSTATE = 128
HEADS = 64
SEQ = 128
INNER = 4096
MAPS = 2 * NSTATE


def from_behind(x, axis, by):
    length = lax.axis_size(axis)
    return lax.ppermute(x, axis, [(i, (i + by) % length) for i in range(length)])


def swap(x, mask):
    length = lax.axis_size("dp")
    return lax.ppermute(x, "dp", [(i, i ^ mask) for i in range(length)])


def masks():
    length = lax.axis_size("dp")
    out = []
    bit = 1
    while bit < length:
        out.append(bit)
        bit *= 2
    return out


def sum_all(x):
    for bit in masks():
        x = x + swap(x, bit)
    return x


def tied(x, other):
    return lax.optimization_barrier((x, other))[0]


def sum_first(part):
    length = lax.axis_size("dp")
    came = {j - 1: swap(part(j).astype(jnp.bfloat16), 1) for j in range(1, length, 2)}
    return {j: part(j) + came[j].astype(jnp.float32) for j in sorted(came, reverse=True)}


def sum_rest(held, after=None):
    first = None
    for bit in masks()[1:]:
        sent = {j: held[j].astype(jnp.bfloat16) for j in held if j & bit}
        if after is not None and first is None:
            sent = {j: tied(x, after) for j, x in sent.items()}
        came = {j ^ bit: swap(x, bit) for j, x in sent.items()}
        if first is None:
            first = came[0]
        held = {j: held[j] + came[j].astype(jnp.float32) for j in came}
    return held[0], first


def sum_both(x):
    me = lax.axis_index("dp")
    odd = (me & 1) != 0
    x = x + swap(x, 1)
    mine = jnp.where(odd, x[SEQ:], x[:SEQ])
    for bit in masks()[1:]:
        mine = mine + swap(mine, bit)
    other = swap(mine, 1)
    return jnp.where(odd, other, mine), jnp.where(odd, mine, other)


def gather_cols(block, after=None):
    me = lax.axis_index("dp")
    length = lax.axis_size("dp")
    if after is not None:
        block = tied(block, after)
    held = [block]
    order = [0]
    first = None
    for bit in reversed(masks()):
        held = held + [swap(b, bit) for b in held]
        order = order + [j ^ bit for j in order]
        if first is None:
            first = held[1]
    by_mask = {j: b for j, b in zip(order, held)}
    level = [by_mask[j] for j in range(length)]
    for bit in masks():
        flip = (me & bit) != 0
        level = [jnp.where(flip, level[j ^ bit], level[j]) for j in range(length)]
    return jnp.concatenate(level, axis=1), first


def causal_conv(values, kernel_taps):
    kernel = kernel_taps.shape[0]
    length = values.shape[0]
    padded = jnp.pad(values, ((kernel - 1, 0), (0, 0)))
    running = jnp.zeros_like(values)
    for offset in range(kernel):
        running = running + kernel_taps[offset] * padded[offset : offset + length]
    return running


def mixer(proj_x, proj_z, proj_dt, scores, conv_taps, dt_offset, log_rate, skip_gain):
    length, width = proj_x.shape
    nheads = dt_offset.shape[0]
    head_width = width // nheads
    xconv = jax.nn.silu(causal_conv(proj_x, conv_taps))
    steps = jax.nn.softplus(proj_dt + dt_offset)
    position = jnp.arange(length)
    causal = position[:, None] >= position[None, :]
    cumul = jnp.dot(
        causal.astype(jnp.float32), steps * -jnp.exp(log_rate), precision=lax.Precision.HIGHEST
    )
    heads_cum = cumul.T
    spread = heads_cum[:, :, None] - heads_cum[:, None, :]
    decay = jnp.where(causal[None], jnp.exp(jnp.where(causal[None], spread, 0.0)), 0.0)
    weights = decay * scores[None] * steps.T[:, None, :]
    heads_in = xconv.reshape(length, nheads, head_width)
    result = jnp.einsum("hts,shp->thp", weights, heads_in, precision=lax.Precision.HIGH)
    result = result + skip_gain[None, :, None] * heads_in
    gate_in = jax.nn.silu(proj_z.reshape(length, nheads, head_width))
    return (result * gate_in).reshape(length, width)


def times_transposed(left, right):
    return lax.dot_general(
        left, right, (((1,), (1,)), ((), ())), preferred_element_type=jnp.float32
    )


def transposed_times(left, right):
    return lax.dot_general(
        left, right, (((0,), (0,)), ((), ())), preferred_element_type=jnp.float32
    )


def per_device(
    act_in,
    saved_act,
    cotangent,
    weight_xz,
    weight_bcdt,
    weight_out,
    conv_x,
    conv_bc,
    dt_bias,
    a_log,
    d_skip,
    norm_gain,
):
    input_rows = act_in[0]
    saved_rows = saved_act[0]
    cot_rows = cotangent[0]
    local_xz = weight_xz[0]
    local_bcdt = weight_bcdt[0]
    local_out = weight_out[0]
    taps_x = conv_x[0]
    taps_bc = conv_bc[0]
    dt_offset = dt_bias[0]
    log_rate = a_log[0]
    skip_gain = d_skip[0]
    gain_local = norm_gain[0]
    own_heads = dt_offset.shape[0]
    me = lax.axis_index("dp")
    head_first = me * own_heads
    width = own_heads * HEAD_DIM

    def whole_act(pre_part):
        return jax.nn.silu(causal_conv(pre_part, taps_bc))

    both = jnp.concatenate([saved_rows, input_rows], axis=0)
    both_values = both.astype(jnp.float32)
    squares = jnp.sum(both_values * both_values, axis=1, keepdims=True)
    back_small, forward_small = sum_both(
        jnp.concatenate([times_transposed(both, local_bcdt), squares], axis=1)
    )

    def xz_part(j):
        cols = lax.dynamic_slice_in_dim(local_xz, (me ^ j) * 2 * width, 2 * width, 1)
        return jnp.dot(both, cols, preferred_element_type=jnp.float32)

    held_xz = sum_first(xz_part)
    back_raw, back_first = sum_rest({j: x[:SEQ] for j, x in held_xz.items()})

    def mixed_part(j):
        taken = lax.dynamic_slice_in_dim(local_out, (me ^ j) * width, width, 0)
        return times_transposed(cot_rows, taken)

    d_mixed, mixed_first = sum_rest(sum_first(mixed_part), back_first)
    forward_raw, forward_first = sum_rest(
        {j: x[SEQ:] for j, x in held_xz.items()}, mixed_first
    )

    def project(rows, small, raw_xz):
        raw_cols = small[:, : MAPS + HEADS]
        scales = lax.rsqrt(small[:, MAPS + HEADS :] / D + 1e-05)
        return (rows.astype(jnp.float32), scales, raw_xz, raw_cols)

    back_proj = project(saved_rows, back_small, back_raw)
    forward_proj = project(input_rows, forward_small, forward_raw)

    def gate_parts(projected):
        values, scales, raw_xz, raw_cols = projected
        own_xz = raw_xz * scales
        whole_cols = raw_cols * scales
        pre_part = whole_cols[:, :MAPS]
        maps = whole_act(pre_part).astype(jnp.bfloat16)
        own_dt = lax.dynamic_slice_in_dim(whole_cols[:, MAPS:], head_first, own_heads, 1)
        split_xz = own_xz.reshape(SEQ, own_heads, 2, HEAD_DIM)
        mix_x = split_xz[:, :, 0].reshape(SEQ, width)
        mix_z = split_xz[:, :, 1].reshape(SEQ, width)
        scores = times_transposed(maps[:, NSTATE:], maps[:, :NSTATE])

        def local_mix(in_x, in_z, in_dt, in_scores):
            return mixer(in_x, in_z, in_dt, in_scores, taps_x, dt_offset, log_rate, skip_gain)

        gated, mix_back = jax.vjp(local_mix, mix_x, mix_z, own_dt, scores)
        return (gated, mix_back, maps, pre_part)

    values, scales, raw_xz, raw_cols = back_proj
    gated, mix_back, maps, pre_part = gate_parts(back_proj)
    gained = gated * gain_local
    row_sums = sum_all(
        jnp.stack([jnp.sum(gated * gated, axis=1), jnp.sum(d_mixed * gained, axis=1)])
    )
    inverse = lax.rsqrt(row_sums[0] / INNER + 1e-05)[:, None]
    dots = row_sums[1][:, None]
    mixed_in = (gained * inverse).astype(jnp.bfloat16)
    d_gated = inverse * gain_local * d_mixed - gated * (inverse * inverse * inverse) * dots / INNER
    d_px, d_pz, d_pdt, d_scores = mix_back(d_gated)
    own_round = (
        jnp.stack(
            [
                d_px.reshape(SEQ, own_heads, HEAD_DIM),
                d_pz.reshape(SEQ, own_heads, HEAD_DIM),
            ],
            axis=2,
        )
        .reshape(SEQ, own_heads * 2 * HEAD_DIM)
        .astype(jnp.bfloat16)
    )
    round_xz, round_first = gather_cols(own_round)
    inner_own = jnp.sum(own_round.astype(jnp.float32) * raw_xz, axis=1, keepdims=True)
    wide_maps = maps.astype(jnp.float32)
    d_maps = jnp.concatenate(
        [
            jnp.dot(d_scores.T, wide_maps[:, NSTATE:], precision=lax.Precision.HIGH),
            jnp.dot(d_scores, wide_maps[:, :NSTATE], precision=lax.Precision.HIGH),
        ],
        axis=1,
    )
    d_dt_full = lax.dynamic_update_slice_in_dim(
        jnp.zeros((SEQ, HEADS), jnp.float32), d_pdt, head_first, 1
    )
    summed = sum_all(jnp.concatenate([d_maps, d_dt_full, inner_own], axis=1))
    conv_out, conv_back = jax.vjp(whole_act, pre_part)
    d_pre = conv_back(summed[:, :MAPS])[0]
    round_bcdt = jnp.concatenate([d_pre, summed[:, MAPS : MAPS + HEADS]], axis=1).astype(
        jnp.bfloat16
    )
    inner_sum = summed[:, MAPS + HEADS :] + jnp.sum(
        round_bcdt.astype(jnp.float32) * raw_cols, axis=1, keepdims=True
    )

    fwd_gated = gate_parts(forward_proj)[0]
    fwd_all, _ = gather_cols((fwd_gated * gain_local).astype(jnp.bfloat16), round_first)
    fwd_sum = sum_all(jnp.sum(fwd_gated * fwd_gated, axis=1)[None])
    fwd_inverse = lax.rsqrt(fwd_sum[0] / INNER + 1e-05)[:, None]
    mixed = jnp.dot(fwd_all, local_out, preferred_element_type=jnp.float32) * fwd_inverse
    section_out = (input_rows.astype(jnp.float32) + mixed).astype(jnp.bfloat16)
    next_act = from_behind(section_out, "section", 1)

    normed = (values * scales).astype(jnp.bfloat16)
    d_normed = times_transposed(round_xz, local_xz)
    d_normed = d_normed + jnp.dot(round_bcdt, local_bcdt, preferred_element_type=jnp.float32)
    d_norm_in = scales * d_normed - values * (scales * scales * scales) * inner_sum / D
    d_input = (cot_rows.astype(jnp.float32) + d_norm_in).astype(jnp.bfloat16)
    prev_grad = from_behind(d_input, "section", -1)

    grad_out = transposed_times(gather_cols(mixed_in, round_first)[0], cot_rows)
    grad_xz = transposed_times(normed, round_xz)
    grad_bcdt = transposed_times(round_bcdt, normed)
    return (next_act[None], prev_grad[None], grad_xz[None], grad_bcdt[None], grad_out[None])


def solution(mesh):
    return jax.shard_map(
        per_device,
        mesh=mesh,
        in_specs=(
            P("section", None, "dp"),
            P("section", None, "dp"),
            P("section", None, "dp"),
            P("section", "dp", None),
            P("section", None, "dp"),
            P("section", None, "dp"),
            P("section", None, "dp"),
            P("section", None, None),
            P("section", "dp"),
            P("section", "dp"),
            P("section", "dp"),
            P("section", "dp"),
        ),
        out_specs=(
            P("section", None, "dp"),
            P("section", None, "dp"),
            P("section", "dp", None),
            P("section", None, "dp"),
            P("section", None, "dp"),
        ),
        check_vma=False,
    )
```

```python
import jax
import jax.numpy as jnp
from jax import lax
from jax.sharding import PartitionSpec as P

D = 2048
HEAD_DIM = 64
NSTATE = 128
HEADS = 64
SEQ = 128
INNER = 4096
MAPS = 2 * NSTATE


def from_behind(x, axis, by):
    length = lax.axis_size(axis)
    return lax.ppermute(x, axis, [(i, (i + by) % length) for i in range(length)])


def swap(x, mask):
    length = lax.axis_size("dp")
    return lax.ppermute(x, "dp", [(i, i ^ mask) for i in range(length)])


def masks():
    length = lax.axis_size("dp")
    out = []
    bit = 1
    while bit < length:
        out.append(bit)
        bit *= 2
    return out


def sum_all(x):
    for bit in masks():
        x = x + swap(x, bit)
    return x


def tied(x, other):
    return lax.optimization_barrier((x, other))[0]


def sum_first(part):
    length = lax.axis_size("dp")
    came = {j - 1: swap(part(j).astype(jnp.bfloat16), 1) for j in range(1, length, 2)}
    return {j: part(j) + came[j].astype(jnp.float32) for j in sorted(came, reverse=True)}


def sum_rest(held, after=None):
    first = begun = None
    for bit in masks()[1:]:
        sent = {j: held[j].astype(jnp.bfloat16) for j in held if j & bit}
        if after is not None and first is None:
            sent = {j: tied(x, after) for j, x in sent.items()}
        came = {j ^ bit: swap(x, bit) for j, x in sent.items()}
        if first is None:
            first = came[0]
            begun = sent[bit]
        held = {j: held[j] + came[j].astype(jnp.float32) for j in came}
    return held[0], first, begun


def sum_both(x, after):
    me = lax.axis_index("dp")
    odd = (me & 1) != 0
    x = x + swap(x, 1)
    mine = tied(jnp.where(odd, x[SEQ:], x[:SEQ]), after)
    for bit in masks()[1:]:
        mine = mine + swap(mine, bit)
    other = swap(mine, 1)
    return jnp.where(odd, other, mine), jnp.where(odd, mine, other)


def gather_cols(block, after=None):
    me = lax.axis_index("dp")
    length = lax.axis_size("dp")
    if after is not None:
        block = tied(block, after)
    held = [block]
    order = [0]
    for bit in reversed(masks()):
        held = held + [swap(b, bit) for b in held]
        order = order + [j ^ bit for j in order]
    by_mask = {j: b for j, b in zip(order, held)}
    level = [by_mask[j] for j in range(length)]
    for bit in masks():
        flip = (me & bit) != 0
        level = [jnp.where(flip, level[j ^ bit], level[j]) for j in range(length)]
    return jnp.concatenate(level, axis=1), held[-1]


def causal_conv(values, kernel_taps):
    kernel = kernel_taps.shape[0]
    length = values.shape[0]
    padded = jnp.pad(values, ((kernel - 1, 0), (0, 0)))
    running = jnp.zeros_like(values)
    for offset in range(kernel):
        running = running + kernel_taps[offset] * padded[offset : offset + length]
    return running


def mixer(proj_x, proj_z, proj_dt, scores, conv_taps, dt_offset, log_rate, skip_gain):
    length, width = proj_x.shape
    nheads = dt_offset.shape[0]
    head_width = width // nheads
    xconv = jax.nn.silu(causal_conv(proj_x, conv_taps))
    steps = jax.nn.softplus(proj_dt + dt_offset)
    position = jnp.arange(length)
    causal = position[:, None] >= position[None, :]
    cumul = jnp.dot(
        causal.astype(jnp.float32), steps * -jnp.exp(log_rate), precision=lax.Precision.HIGHEST
    )
    heads_cum = cumul.T
    spread = heads_cum[:, :, None] - heads_cum[:, None, :]
    decay = jnp.where(causal[None], jnp.exp(jnp.where(causal[None], spread, 0.0)), 0.0)
    weights = decay * scores[None] * steps.T[:, None, :]
    heads_in = xconv.reshape(length, nheads, head_width)
    result = jnp.einsum("hts,shp->thp", weights, heads_in, precision=lax.Precision.HIGH)
    result = result + skip_gain[None, :, None] * heads_in
    gate_in = jax.nn.silu(proj_z.reshape(length, nheads, head_width))
    return (result * gate_in).reshape(length, width)


def times_transposed(left, right):
    return lax.dot_general(
        left, right, (((1,), (1,)), ((), ())), preferred_element_type=jnp.float32
    )


def transposed_times(left, right):
    return lax.dot_general(
        left, right, (((0,), (0,)), ((), ())), preferred_element_type=jnp.float32
    )


def per_device(
    act_in,
    saved_act,
    cotangent,
    weight_xz,
    weight_bcdt,
    weight_out,
    conv_x,
    conv_bc,
    dt_bias,
    a_log,
    d_skip,
    norm_gain,
):
    input_rows = act_in[0]
    saved_rows = saved_act[0]
    cot_rows = cotangent[0]
    local_xz = weight_xz[0]
    local_bcdt = weight_bcdt[0]
    local_out = weight_out[0]
    taps_x = conv_x[0]
    taps_bc = conv_bc[0]
    dt_offset = dt_bias[0]
    log_rate = a_log[0]
    skip_gain = d_skip[0]
    gain_local = norm_gain[0]
    own_heads = dt_offset.shape[0]
    me = lax.axis_index("dp")
    head_first = me * own_heads
    width = own_heads * HEAD_DIM

    def whole_act(pre_part):
        return jax.nn.silu(causal_conv(pre_part, taps_bc))

    both = jnp.concatenate([saved_rows, input_rows], axis=0)
    both_values = both.astype(jnp.float32)
    squares = jnp.sum(both_values * both_values, axis=1, keepdims=True)
    def xz_part(j):
        cols = lax.dynamic_slice_in_dim(local_xz, (me ^ j) * 2 * width, 2 * width, 1)
        return jnp.dot(both, cols, preferred_element_type=jnp.float32)

    held_xz = sum_first(xz_part)
    back_raw, back_first, back_begun = sum_rest({j: x[:SEQ] for j, x in held_xz.items()})
    back_small, forward_small = sum_both(
        jnp.concatenate([times_transposed(both, local_bcdt), squares], axis=1), back_begun
    )

    def mixed_part(j):
        taken = lax.dynamic_slice_in_dim(local_out, (me ^ j) * width, width, 0)
        return times_transposed(cot_rows, taken)

    d_mixed = sum_rest(sum_first(mixed_part), back_begun)[0]
    forward_raw = sum_rest({j: x[SEQ:] for j, x in held_xz.items()}, back_first)[0]

    def project(rows, small, raw_xz):
        raw_cols = small[:, : MAPS + HEADS]
        scales = lax.rsqrt(small[:, MAPS + HEADS :] / D + 1e-05)
        return (rows.astype(jnp.float32), scales, raw_xz, raw_cols)

    back_proj = project(saved_rows, back_small, back_raw)
    forward_proj = project(input_rows, forward_small, forward_raw)

    def gate_parts(projected):
        values, scales, raw_xz, raw_cols = projected
        own_xz = raw_xz * scales
        whole_cols = raw_cols * scales
        pre_part = whole_cols[:, :MAPS]
        maps = whole_act(pre_part).astype(jnp.bfloat16)
        own_dt = lax.dynamic_slice_in_dim(whole_cols[:, MAPS:], head_first, own_heads, 1)
        split_xz = own_xz.reshape(SEQ, own_heads, 2, HEAD_DIM)
        mix_x = split_xz[:, :, 0].reshape(SEQ, width)
        mix_z = split_xz[:, :, 1].reshape(SEQ, width)
        scores = times_transposed(maps[:, NSTATE:], maps[:, :NSTATE])

        def local_mix(in_x, in_z, in_dt, in_scores):
            return mixer(in_x, in_z, in_dt, in_scores, taps_x, dt_offset, log_rate, skip_gain)

        gated, mix_back = jax.vjp(local_mix, mix_x, mix_z, own_dt, scores)
        return (gated, mix_back, maps, pre_part)

    values, scales, raw_xz, raw_cols = back_proj
    gated, mix_back, maps, pre_part = gate_parts(back_proj)
    gained = gated * gain_local
    row_sums = sum_all(
        jnp.stack([jnp.sum(gated * gated, axis=1), jnp.sum(d_mixed * gained, axis=1)])
    )
    inverse = lax.rsqrt(row_sums[0] / INNER + 1e-05)[:, None]
    dots = row_sums[1][:, None]
    mixed_in = (gained * inverse).astype(jnp.bfloat16)
    d_gated = inverse * gain_local * d_mixed - gated * (inverse * inverse * inverse) * dots / INNER
    d_px, d_pz, d_pdt, d_scores = mix_back(d_gated)
    own_round = (
        jnp.stack(
            [
                d_px.reshape(SEQ, own_heads, HEAD_DIM),
                d_pz.reshape(SEQ, own_heads, HEAD_DIM),
            ],
            axis=2,
        )
        .reshape(SEQ, own_heads * 2 * HEAD_DIM)
        .astype(jnp.bfloat16)
    )
    round_xz, round_last = gather_cols(own_round)
    inner_own = jnp.sum(own_round.astype(jnp.float32) * raw_xz, axis=1, keepdims=True)
    wide_maps = maps.astype(jnp.float32)
    d_maps = jnp.concatenate(
        [
            jnp.dot(d_scores.T, wide_maps[:, NSTATE:], precision=lax.Precision.HIGH),
            jnp.dot(d_scores, wide_maps[:, :NSTATE], precision=lax.Precision.HIGH),
        ],
        axis=1,
    )
    d_dt_full = lax.dynamic_update_slice_in_dim(
        jnp.zeros((SEQ, HEADS), jnp.float32), d_pdt, head_first, 1
    )
    summed = sum_all(jnp.concatenate([d_maps, d_dt_full, inner_own], axis=1))
    conv_out, conv_back = jax.vjp(whole_act, pre_part)
    d_pre = conv_back(summed[:, :MAPS])[0]
    round_bcdt = jnp.concatenate([d_pre, summed[:, MAPS : MAPS + HEADS]], axis=1).astype(
        jnp.bfloat16
    )
    inner_sum = summed[:, MAPS + HEADS :] + jnp.sum(
        round_bcdt.astype(jnp.float32) * raw_cols, axis=1, keepdims=True
    )

    fwd_gated = gate_parts(forward_proj)[0]
    fwd_all, _ = gather_cols((fwd_gated * gain_local).astype(jnp.bfloat16), round_last)
    fwd_sum = sum_all(jnp.sum(fwd_gated * fwd_gated, axis=1)[None])
    fwd_inverse = lax.rsqrt(fwd_sum[0] / INNER + 1e-05)[:, None]
    mixed = jnp.dot(fwd_all, local_out, preferred_element_type=jnp.float32) * fwd_inverse
    section_out = (input_rows.astype(jnp.float32) + mixed).astype(jnp.bfloat16)
    next_act = from_behind(section_out, "section", 1)

    normed = (values * scales).astype(jnp.bfloat16)
    d_normed = times_transposed(round_xz, local_xz)
    d_normed = d_normed + jnp.dot(round_bcdt, local_bcdt, preferred_element_type=jnp.float32)
    d_norm_in = scales * d_normed - values * (scales * scales * scales) * inner_sum / D
    d_input = (cot_rows.astype(jnp.float32) + d_norm_in).astype(jnp.bfloat16)
    prev_grad = from_behind(d_input, "section", -1)

    grad_out = transposed_times(gather_cols(mixed_in, round_last)[0], cot_rows)
    grad_xz = transposed_times(normed, round_xz)
    grad_bcdt = transposed_times(round_bcdt, normed)
    return (next_act[None], prev_grad[None], grad_xz[None], grad_bcdt[None], grad_out[None])


def solution(mesh):
    return jax.shard_map(
        per_device,
        mesh=mesh,
        in_specs=(
            P("section", None, "dp"),
            P("section", None, "dp"),
            P("section", None, "dp"),
            P("section", "dp", None),
            P("section", None, "dp"),
            P("section", None, "dp"),
            P("section", None, "dp"),
            P("section", None, None),
            P("section", "dp"),
            P("section", "dp"),
            P("section", "dp"),
            P("section", "dp"),
        ),
        out_specs=(
            P("section", None, "dp"),
            P("section", None, "dp"),
            P("section", "dp", None),
            P("section", None, "dp"),
            P("section", None, "dp"),
        ),
        check_vma=False,
    )
```

```python
import jax
import jax.numpy as jnp
from jax import lax
from jax.sharding import PartitionSpec as P

D = 2048
HEAD_DIM = 64
NSTATE = 128
HEADS = 64
SEQ = 128
INNER = 4096
MAPS = 2 * NSTATE


def from_behind(x, axis, by):
    length = lax.axis_size(axis)
    return lax.ppermute(x, axis, [(i, (i + by) % length) for i in range(length)])


def swap(x, mask):
    length = lax.axis_size("dp")
    return lax.ppermute(x, "dp", [(i, i ^ mask) for i in range(length)])


def masks():
    length = lax.axis_size("dp")
    out = []
    bit = 1
    while bit < length:
        out.append(bit)
        bit *= 2
    return out


def sum_all(x):
    for bit in masks():
        x = x + swap(x, bit)
    return x


def tied(x, other):
    return lax.optimization_barrier((x, other))[0]


def sum_first(part):
    length = lax.axis_size("dp")
    came = {j - 1: swap(part(j).astype(jnp.bfloat16), 1) for j in range(1, length, 2)}
    return {j: part(j) + came[j].astype(jnp.float32) for j in sorted(came, reverse=True)}


def sum_rest(held, after=None):
    first = begun = None
    for bit in masks()[1:]:
        sent = {j: held[j].astype(jnp.bfloat16) for j in held if j & bit}
        if after is not None and first is None:
            sent = {j: tied(x, after) for j, x in sent.items()}
        came = {j ^ bit: swap(x, bit) for j, x in sent.items()}
        if first is None:
            first = came[0]
            begun = sent[bit]
        held = {j: held[j] + came[j].astype(jnp.float32) for j in came}
    return held[0], first, begun


def sum_both(x, after):
    me = lax.axis_index("dp")
    odd = (me & 1) != 0
    x = x + swap(x, 1)
    mine = tied(jnp.where(odd, x[SEQ:], x[:SEQ]), after)
    for bit in masks()[1:]:
        mine = mine + swap(mine, bit)
    other = swap(mine, 1)
    return jnp.where(odd, other, mine), jnp.where(odd, mine, other)


def gather_cols(block, after=None):
    me = lax.axis_index("dp")
    length = lax.axis_size("dp")
    if after is not None:
        block = tied(block, after)
    held = [block]
    order = [0]
    for bit in reversed(masks()):
        held = held + [swap(b, bit) for b in held]
        order = order + [j ^ bit for j in order]
    by_mask = {j: b for j, b in zip(order, held)}
    level = [by_mask[j] for j in range(length)]
    for bit in masks():
        flip = (me & bit) != 0
        level = [jnp.where(flip, level[j ^ bit], level[j]) for j in range(length)]
    return jnp.concatenate(level, axis=1), held[-1]


def causal_conv(values, kernel_taps):
    kernel = kernel_taps.shape[0]
    length = values.shape[0]
    padded = jnp.pad(values, ((kernel - 1, 0), (0, 0)))
    running = jnp.zeros_like(values)
    for offset in range(kernel):
        running = running + kernel_taps[offset] * padded[offset : offset + length]
    return running


def mixer(proj_x, proj_z, proj_dt, scores, conv_taps, dt_offset, log_rate, skip_gain):
    length, width = proj_x.shape
    nheads = dt_offset.shape[0]
    head_width = width // nheads
    xconv = jax.nn.silu(causal_conv(proj_x, conv_taps))
    steps = jax.nn.softplus(proj_dt + dt_offset)
    position = jnp.arange(length)
    causal = position[:, None] >= position[None, :]
    cumul = jnp.dot(
        causal.astype(jnp.float32), steps * -jnp.exp(log_rate), precision=lax.Precision.HIGHEST
    )
    heads_cum = cumul.T
    spread = heads_cum[:, :, None] - heads_cum[:, None, :]
    decay = jnp.where(causal[None], jnp.exp(jnp.where(causal[None], spread, 0.0)), 0.0)
    weights = decay * scores[None] * steps.T[:, None, :]
    heads_in = xconv.reshape(length, nheads, head_width)
    result = jnp.einsum("hts,shp->thp", weights, heads_in, precision=lax.Precision.HIGH)
    result = result + skip_gain[None, :, None] * heads_in
    gate_in = jax.nn.silu(proj_z.reshape(length, nheads, head_width))
    return (result * gate_in).reshape(length, width)


def times_transposed(left, right):
    return lax.dot_general(
        left, right, (((1,), (1,)), ((), ())), preferred_element_type=jnp.float32
    )


def transposed_times(left, right):
    return lax.dot_general(
        left, right, (((0,), (0,)), ((), ())), preferred_element_type=jnp.float32
    )


def per_device(
    act_in,
    saved_act,
    cotangent,
    weight_xz,
    weight_bcdt,
    weight_out,
    conv_x,
    conv_bc,
    dt_bias,
    a_log,
    d_skip,
    norm_gain,
):
    input_rows = act_in[0]
    saved_rows = saved_act[0]
    cot_rows = cotangent[0]
    local_xz = weight_xz[0]
    local_bcdt = weight_bcdt[0]
    local_out = weight_out[0]
    taps_x = conv_x[0]
    taps_bc = conv_bc[0]
    dt_offset = dt_bias[0]
    log_rate = a_log[0]
    skip_gain = d_skip[0]
    gain_local = norm_gain[0]
    own_heads = dt_offset.shape[0]
    me = lax.axis_index("dp")
    head_first = me * own_heads
    width = own_heads * HEAD_DIM

    def whole_act(pre_part):
        return jax.nn.silu(causal_conv(pre_part, taps_bc))

    both = jnp.concatenate([saved_rows, input_rows], axis=0)
    both_values = both.astype(jnp.float32)
    squares = jnp.sum(both_values * both_values, axis=1, keepdims=True)
    def xz_part(j):
        cols = lax.dynamic_slice_in_dim(local_xz, (me ^ j) * 2 * width, 2 * width, 1)
        return jnp.dot(both, cols, preferred_element_type=jnp.float32)

    held_xz = sum_first(xz_part)
    back_raw, back_first, back_begun = sum_rest({j: x[:SEQ] for j, x in held_xz.items()})
    back_small, forward_small = sum_both(
        jnp.concatenate([times_transposed(both, local_bcdt), squares], axis=1), back_begun
    )

    def mixed_part(j):
        taken = lax.dynamic_slice_in_dim(local_out, (me ^ j) * width, width, 0)
        return times_transposed(cot_rows, taken)

    d_mixed = sum_rest(sum_first(mixed_part), back_begun)[0]
    forward_raw = sum_rest({j: x[SEQ:] for j, x in held_xz.items()}, back_first)[0]

    def project(rows, small, raw_xz):
        raw_cols = small[:, : MAPS + HEADS]
        scales = lax.rsqrt(small[:, MAPS + HEADS :] / D + 1e-05)
        return (rows.astype(jnp.float32), scales, raw_xz, raw_cols)

    back_proj = project(saved_rows, back_small, back_raw)
    forward_proj = project(input_rows, forward_small, forward_raw)

    def gate_parts(projected):
        values, scales, raw_xz, raw_cols = projected
        own_xz = raw_xz * scales
        whole_cols = raw_cols * scales
        pre_part = whole_cols[:, :MAPS]
        maps = whole_act(pre_part).astype(jnp.bfloat16)
        own_dt = lax.dynamic_slice_in_dim(whole_cols[:, MAPS:], head_first, own_heads, 1)
        split_xz = own_xz.reshape(SEQ, own_heads, 2, HEAD_DIM)
        mix_x = split_xz[:, :, 0].reshape(SEQ, width)
        mix_z = split_xz[:, :, 1].reshape(SEQ, width)
        scores = times_transposed(maps[:, NSTATE:], maps[:, :NSTATE])

        def local_mix(in_x, in_z, in_dt, in_scores):
            return mixer(in_x, in_z, in_dt, in_scores, taps_x, dt_offset, log_rate, skip_gain)

        gated, mix_back = jax.vjp(local_mix, mix_x, mix_z, own_dt, scores)
        return (gated, mix_back, maps, pre_part)

    values, scales, raw_xz, raw_cols = back_proj
    gated, mix_back, maps, pre_part = gate_parts(back_proj)
    gained = gated * gain_local
    row_sums = sum_all(
        jnp.stack([jnp.sum(gated * gated, axis=1), jnp.sum(d_mixed * gained, axis=1)])
    )
    inverse = lax.rsqrt(row_sums[0] / INNER + 1e-05)[:, None]
    dots = row_sums[1][:, None]
    mixed_in = (gained * inverse).astype(jnp.bfloat16)
    d_gated = inverse * gain_local * d_mixed - gated * (inverse * inverse * inverse) * dots / INNER
    d_px, d_pz, d_pdt, d_scores = mix_back(d_gated)
    own_round = (
        jnp.stack(
            [
                d_px.reshape(SEQ, own_heads, HEAD_DIM),
                d_pz.reshape(SEQ, own_heads, HEAD_DIM),
            ],
            axis=2,
        )
        .reshape(SEQ, own_heads * 2 * HEAD_DIM)
        .astype(jnp.bfloat16)
    )
    round_xz, round_last = gather_cols(own_round)
    inner_own = jnp.sum(own_round.astype(jnp.float32) * raw_xz, axis=1, keepdims=True)
    wide_maps = maps.astype(jnp.float32)
    d_maps = jnp.concatenate(
        [
            jnp.dot(d_scores.T, wide_maps[:, NSTATE:], precision=lax.Precision.HIGH),
            jnp.dot(d_scores, wide_maps[:, :NSTATE], precision=lax.Precision.HIGH),
        ],
        axis=1,
    )
    d_dt_full = lax.dynamic_update_slice_in_dim(
        jnp.zeros((SEQ, HEADS), jnp.float32), d_pdt, head_first, 1
    )
    map_part = jnp.concatenate([d_maps, d_dt_full, inner_own], axis=1)
    summed = sum_all(map_part)
    conv_out, conv_back = jax.vjp(whole_act, pre_part)
    d_pre = conv_back(summed[:, :MAPS])[0]
    round_bcdt = jnp.concatenate([d_pre, summed[:, MAPS : MAPS + HEADS]], axis=1).astype(
        jnp.bfloat16
    )
    inner_sum = summed[:, MAPS + HEADS :] + jnp.sum(
        round_bcdt.astype(jnp.float32) * raw_cols, axis=1, keepdims=True
    )

    late_raw = tied(forward_proj[2], map_part)
    fwd_gated = gate_parts(forward_proj[:2] + (late_raw,) + forward_proj[3:])[0]
    fwd_all, _ = gather_cols((fwd_gated * gain_local).astype(jnp.bfloat16), round_last)
    fwd_sum = sum_all(jnp.sum(fwd_gated * fwd_gated, axis=1)[None])
    fwd_inverse = lax.rsqrt(fwd_sum[0] / INNER + 1e-05)[:, None]
    mixed = jnp.dot(fwd_all, local_out, preferred_element_type=jnp.float32) * fwd_inverse
    section_out = (input_rows.astype(jnp.float32) + mixed).astype(jnp.bfloat16)
    next_act = from_behind(section_out, "section", 1)

    normed = (values * scales).astype(jnp.bfloat16)
    d_normed = times_transposed(round_xz, local_xz)
    d_normed = d_normed + jnp.dot(round_bcdt, local_bcdt, preferred_element_type=jnp.float32)
    d_norm_in = scales * d_normed - values * (scales * scales * scales) * inner_sum / D
    d_input = (cot_rows.astype(jnp.float32) + d_norm_in).astype(jnp.bfloat16)
    prev_grad = from_behind(d_input, "section", -1)

    grad_out = transposed_times(gather_cols(mixed_in, round_last)[0], cot_rows)
    grad_xz = transposed_times(normed, round_xz)
    grad_bcdt = transposed_times(round_bcdt, normed)
    return (next_act[None], prev_grad[None], grad_xz[None], grad_bcdt[None], grad_out[None])


def solution(mesh):
    return jax.shard_map(
        per_device,
        mesh=mesh,
        in_specs=(
            P("section", None, "dp"),
            P("section", None, "dp"),
            P("section", None, "dp"),
            P("section", "dp", None),
            P("section", None, "dp"),
            P("section", None, "dp"),
            P("section", None, "dp"),
            P("section", None, None),
            P("section", "dp"),
            P("section", "dp"),
            P("section", "dp"),
            P("section", "dp"),
        ),
        out_specs=(
            P("section", None, "dp"),
            P("section", None, "dp"),
            P("section", "dp", None),
            P("section", None, "dp"),
            P("section", None, "dp"),
        ),
        check_vma=False,
    )
```
